32 devices in a mesh: grp: 2 (over x), dev: 16 (over z, y, core).
Axes of the slice: x: 2, y: 2, z: 4, core: 2. Of those that a mesh axis runs over, the one named last changes fastest.
Arguments:
- coords: float32 [16384, 64], P(('grp', 'dev')), may hold values from -6 to 6
- right_side: float32 [16384, 256], P(('grp', 'dev')), may hold values from -6 to 6
- leaf_perm: int32 [32, 512], P(('grp', 'dev')), may hold values from 0 to 511, each once within a row
- near_list: int32 [32, 4], P(('grp', 'dev')), may hold values from -1 to 31, as said below
- far_leaves: int32 [32, 4], P(('grp', 'dev')), may hold values from 0 to 31, as said below
- couplings: bfloat16 [32, 4, 128, 128], P(('grp', 'dev')), may hold values from -0.5 to 0.5
- transfer: bfloat16 [32, 128, 128], P(('grp', 'dev')), may hold values from -0.5 to 0.5
- leaf_basis: bfloat16 [16384, 128], P(('grp', 'dev')), may hold values from -0.25 to 0.25
- cluster_of: int32 [32], P(('grp', 'dev')), may hold values from 0 to 7, as said below
- far_clusters: int32 [8, 4], P('grp'), may hold values from 0 to 7, as said below
- cluster_couplings: bfloat16 [8, 4, 128, 128], P('grp'), may hold values from -0.25 to 0.25
- ridge_weight: float32 [], replicated, may hold values from 0.5 to 2
Outputs:
- solution: float32 [16384, 256], P(('grp', 'dev'))
- residual: float32 [16384, 256], P(('grp', 'dev'))
The draws below stay inside these ranges and needn't reach their ends.
Inputs may be any that keep to these rules, and one draw needn't show every extreme that they name: `near_list`: each row lists leaves of the row's group whose position within the group differs from the row's leaf by 1 to 2, each at most once, in any slot order; -1 marks an empty slot. The number of listed leaves varies from leaf to leaf. `far_leaves`: each row names 4 different leaves of the row's group whose position within the group differs from the row's leaf by more than 2 and at most 8. `cluster_of`: leaves of group g belong to clusters g * 4 to g * 4 + 3, and every cluster holds exactly 4 leaves. `far_clusters`: each row names 4 different clusters, none of them in the row's own group.
All inputs are finite; a program needn't handle non-finite values.
Results may differ from the reference program's by a relative error of at most 0.0033.
Values may be sent and summed in bfloat16 or wider, within the bound.
A program may use at most 64 MiB of HBM per device.

```python
import jax
import jax.numpy as jnp
from jax import lax

LEAF = 512
DIM = 64
OUT = 256
RANK = 128
REACH = 2
FARREACH = 8
FAR1 = 4
FAR2 = 4
CPG = 4
ITERS = 2
LEAVES = 32
POINTS = 16384
CLUS = 8
LPC = 4
N_GRP = 2
N_DEV = 16


def draw_near_list(key, part):
    count_all = N_GRP * N_DEV
    offset_table = jnp.concatenate([jnp.arange(-REACH, 0), jnp.arange(1, REACH + 1)]).astype(jnp.int32)
    subkeys = jax.random.split(key, 3)
    orders = jax.vmap(lambda single: jax.random.permutation(single, 2 * REACH))(jax.random.split(subkeys[0], count_all))
    offsets = offset_table[orders]
    keep_level = jax.random.randint(subkeys[1], (count_all, 1), 1, 5)
    coin_draws = jax.random.randint(subkeys[2], (count_all, 2 * REACH), 0, 4)
    leaf_index = jnp.arange(count_all, dtype=jnp.int32)[:, None]
    position = leaf_index % N_DEV + offsets
    retained = (coin_draws < keep_level) & (position >= 0) & (position < N_DEV)
    return jnp.where(retained, leaf_index + offsets, -1).astype(jnp.int32)


def draw_far_leaves(key, part):
    count_all = N_GRP * N_DEV
    orders = jax.vmap(lambda single: jax.random.permutation(single, N_DEV))(jax.random.split(jax.random.fold_in(key, 11), count_all))
    leaf_index = jnp.arange(count_all, dtype=jnp.int32)[:, None]
    offset = orders - leaf_index % N_DEV
    allowed = (jnp.abs(offset) > REACH) & (jnp.abs(offset) <= FARREACH)
    ranking = jnp.where(allowed, 0, N_DEV) + jnp.arange(N_DEV, dtype=jnp.int32)[None, :]
    chosen = jnp.argsort(ranking, axis=1)[:, :FAR1]
    picked = jnp.take_along_axis(orders, chosen, axis=1)
    return (leaf_index // N_DEV * N_DEV + picked).astype(jnp.int32)


def draw_cluster_of(key, part):
    per_cluster = N_DEV // CPG
    orders = jax.vmap(lambda single: jax.random.permutation(single, N_DEV))(jax.random.split(jax.random.fold_in(key, 23), N_GRP))
    group_index = jnp.arange(N_GRP, dtype=jnp.int32)[:, None]
    return (group_index * CPG + orders // per_cluster).reshape(N_GRP * N_DEV).astype(jnp.int32)


def draw_far_clusters(key, part):
    count_all = N_GRP * CPG
    orders = jax.vmap(lambda single: jax.random.permutation(single, count_all))(jax.random.split(jax.random.fold_in(key, 37), count_all))
    cluster_index = jnp.arange(count_all, dtype=jnp.int32)[:, None]
    allowed = orders // CPG != cluster_index // CPG
    ranking = jnp.where(allowed, 0, count_all) + jnp.arange(count_all, dtype=jnp.int32)[None, :]
    chosen = jnp.argsort(ranking, axis=1)[:, :FAR2]
    return jnp.take_along_axis(orders, chosen, axis=1).astype(jnp.int32)


def shard_levels(stream_key, extent, cuts, low, largest):
    def one(axis_at, blocks):
        draws = jax.random.uniform(jax.random.fold_in(jax.random.fold_in(stream_key, 6), axis_at), (blocks,), jnp.float32, low / len(cuts), largest / len(cuts))
        return jnp.repeat(jnp.exp(draws), extent[axis_at] // blocks).reshape((-1,) + (1,) * (len(extent) - axis_at - 1))

    level = one(*cuts[0])
    for cut in cuts[1:]:
        level = level * one(*cut)
    return level


def gaussian(key, shape, width, limit, shards=(), held_as=jnp.bfloat16):
    drawn = jax.random.normal(key, shape, jnp.float32) * width
    if len(shards) > 0:
        drawn = shard_levels(key, shape, shards, -0.22, 0.18) * drawn
    return jnp.clip(drawn, min=-limit, max=limit).astype(held_as)


def setup_inputs(seed: int = 0) -> dict:
    streams_of = jax.random.split(jax.random.key(seed), 13)
    return {
        "coords": gaussian(streams_of[0], (POINTS, DIM), 1.0, 6.0, ((0, 32),), jnp.float32),
        "right_side": gaussian(streams_of[1], (POINTS, OUT), 1.0, 6.0, ((0, 32),), jnp.float32),
        "leaf_perm": jax.vmap(lambda own: jax.random.permutation(own, LEAF))(jax.random.split(streams_of[2], LEAVES)).reshape((LEAVES, LEAF)).astype(jnp.int32),
        "near_list": draw_near_list(jax.random.fold_in(streams_of[12], 71), 0),
        "far_leaves": draw_far_leaves(jax.random.fold_in(streams_of[12], 71), 0),
        "couplings": gaussian(streams_of[5], (LEAVES, FAR1, RANK, RANK), RANK ** -0.5, 0.5, ((0, 32),)),
        "transfer": gaussian(streams_of[6], (LEAVES, RANK, RANK), RANK ** -0.5, 0.5, ((0, 32),)),
        "leaf_basis": gaussian(streams_of[7], (POINTS, RANK), LEAF ** -0.5, 0.25, ((0, 32),)),
        "cluster_of": draw_cluster_of(jax.random.fold_in(streams_of[12], 71), 0),
        "far_clusters": draw_far_clusters(jax.random.fold_in(streams_of[12], 71), 0),
        "cluster_couplings": gaussian(streams_of[10], (CLUS, FAR2, RANK, RANK), (RANK * LPC) ** -0.5, 0.25, ((0, 2),)),
        "ridge_weight": jnp.clip(jax.random.uniform(streams_of[11], (), jnp.float32, 0.5, 2.0), 0.5, 2.0),
    }


kernel_scale = 1.0 / 32.0
spectrum_gap = 0.5
spectrum_top = 8.0


def kernel_block(left_points, right_points):
    inner_products = jnp.dot(left_points, right_points.T, precision=lax.Precision.HIGHEST, preferred_element_type=jnp.float32)
    distance = jnp.sum(left_points * left_points, axis=1)[:, None] + jnp.sum(right_points * right_points, axis=1)[None, :] - 2.0 * inner_products
    return jnp.exp(-kernel_scale * distance).astype(jnp.bfloat16)


def place_back(tree_rows, ordering):
    return jnp.zeros_like(tree_rows).at[ordering].set(tree_rows)


def apply_operator(direction, coords, leaf_perm, near_list, far_leaves, couplings, transfer, leaf_basis, cluster_of, far_clusters, cluster_couplings, ridge_weight):
    values = direction.astype(jnp.bfloat16).reshape(LEAVES, LEAF, OUT)
    points = coords.reshape(LEAVES, LEAF, DIM)

    def near_leaf(leaf_id):
        own_points = points[leaf_id]
        accumulated = jnp.dot(kernel_block(own_points, own_points), values[leaf_id], preferred_element_type=jnp.float32)
        for offset in list(range(-REACH, 0)) + list(range(1, REACH + 1)):
            neighbour = jnp.clip(leaf_id + offset, 0, LEAVES - 1)
            listed = jnp.any((near_list[leaf_id] == leaf_id + offset) & (near_list[leaf_id] >= 0)).astype(jnp.float32)
            accumulated = accumulated + listed * jnp.dot(kernel_block(own_points, points[neighbour]), values[neighbour], preferred_element_type=jnp.float32)
        return accumulated

    near_field = lax.map(near_leaf, jnp.arange(LEAVES, dtype=jnp.int32))
    ordered = jnp.take_along_axis(values, leaf_perm[:, :, None], axis=1)
    leaf_bases = leaf_basis.reshape(LEAVES, LEAF, RANK).astype(jnp.float32)
    skeleton = jnp.einsum('lpa,lpo->lao', leaf_bases, ordered.astype(jnp.float32)).astype(jnp.bfloat16)
    transfer_wide = transfer.astype(jnp.float32)
    uplift = jnp.einsum('lba,lbo->lao', transfer_wide, skeleton.astype(jnp.float32))
    cluster_sums = jnp.zeros((CLUS, RANK, OUT), jnp.float32).at[cluster_of].add(uplift).astype(jnp.bfloat16)
    picked = cluster_sums[far_clusters]
    coupled = jnp.einsum('ckab,ckbo->cao', cluster_couplings.astype(jnp.float32), picked.astype(jnp.float32)).astype(jnp.bfloat16)
    partners = skeleton[far_leaves]
    level_one = jnp.einsum('lkab,lkbo->lao', couplings.astype(jnp.float32), partners.astype(jnp.float32))
    local_sum = level_one + jnp.einsum('lab,lbo->lao', transfer_wide, coupled[cluster_of].astype(jnp.float32))
    tree_rows = jnp.einsum('lpa,lao->lpo', leaf_bases, local_sum.astype(jnp.bfloat16).astype(jnp.float32))
    far_field = jax.vmap(place_back)(tree_rows, leaf_perm)
    return ridge_weight * direction + (near_field + far_field).reshape(LEAVES * LEAF, OUT)


def reference(coords, right_side, leaf_perm, near_list, far_leaves, couplings, transfer, leaf_basis, cluster_of, far_clusters, cluster_couplings, ridge_weight):
    bottom_edge = ridge_weight + spectrum_gap
    top_edge = ridge_weight + spectrum_top
    centre = (top_edge + bottom_edge) / 2.0
    spread = (top_edge - bottom_edge) / 2.0
    sigma_ratio = centre / spread
    contraction = 1.0 / sigma_ratio
    direction = right_side / centre
    solution = direction
    residual = right_side
    for rounds in range(ITERS):
        residual = residual - apply_operator(direction, coords, leaf_perm, near_list, far_leaves, couplings, transfer, leaf_basis, cluster_of, far_clusters, cluster_couplings, ridge_weight)
        rho_next = 1.0 / (2.0 * sigma_ratio - contraction)
        direction = rho_next * contraction * direction + (2.0 * rho_next / spread) * residual
        solution = solution + direction
        contraction = rho_next
    return solution, residual
```

```python
import functools

import jax
import jax.numpy as jnp
from jax import lax
from jax.experimental import pallas as pl
from jax.experimental.pallas import tpu as pltpu
from jax.sharding import PartitionSpec as P

MESH = pl.DeviceIdType.MESH

REACH = 2
FARREACH = 8
ITERS = 2


kernel_scale = 1.0 / 32.0
spectrum_gap = 0.5
spectrum_top = 8.0


def from_behind(shard, axis, by):
    devices = lax.axis_size(axis)
    pairs = [(i, i + by) for i in range(devices) if 0 <= i + by < devices]
    return lax.ppermute(shard, axis, pairs)


def kernel_block(left_points, right_points):
    inner_products = jnp.dot(
        left_points,
        right_points.T,
        precision=lax.Precision.HIGHEST,
        preferred_element_type=jnp.float32,
    )
    distance = (
        jnp.sum(left_points * left_points, axis=1)[:, None]
        + jnp.sum(right_points * right_points, axis=1)[None, :]
        - 2.0 * inner_products
    )
    return jnp.exp(-kernel_scale * distance).astype(jnp.bfloat16)


def body(
    coords,
    right_side,
    leaf_perm,
    near_list,
    far_leaves,
    couplings,
    transfer,
    leaf_basis,
    cluster_of,
    far_clusters,
    cluster_couplings,
    ridge_weight,
):
    dev_count = lax.axis_size("dev")
    group_index = lax.axis_index("grp")
    leaf_id = group_index * dev_count + lax.axis_index("dev")
    clusters_here = far_clusters.shape[0]
    local_cluster = cluster_of[0] - group_index * clusters_here
    ordering = leaf_perm[0]
    near_offsets = [offset for offset in range(-REACH, REACH + 1) if offset != 0]
    far_offsets = [offset for offset in range(-FARREACH, FARREACH + 1) if abs(offset) > REACH]
    neighbours = [from_behind(coords, "dev", -offset) for offset in near_offsets]
    near_flags = [
        jnp.any((near_list[0] == leaf_id + offset) & (near_list[0] >= 0)).astype(jnp.float32)
        for offset in near_offsets
    ]
    far_hits = jnp.stack(
        [far_leaves[0] == leaf_id + offset for offset in far_offsets], axis=1
    ).astype(jnp.bfloat16)
    own_block = kernel_block(coords, coords)
    near_blocks = [kernel_block(coords, neighbour_points) for neighbour_points in neighbours]
    cluster_slots = (jnp.arange(clusters_here) == local_cluster).astype(jnp.float32)

    def operate(direction):
        values = direction.astype(jnp.bfloat16)
        near_sum = jnp.dot(own_block, values, preferred_element_type=jnp.float32)
        for position in range(len(near_offsets)):
            remote = from_behind(values, "dev", -near_offsets[position])
            block_here = near_blocks[position]
            near_term = near_flags[position] * jnp.dot(
                block_here, remote, preferred_element_type=jnp.float32
            )
            near_sum = near_sum + near_term
        skeleton = lax.dot_general(
            leaf_basis,
            values[ordering],
            (((0,), (0,)), ((), ())),
            preferred_element_type=jnp.float32,
        ).astype(jnp.bfloat16)
        remote_skeletons = jnp.stack(
            [from_behind(skeleton, "dev", -offset) for offset in far_offsets]
        )
        chosen = jnp.einsum(
            "kj,jbo->kbo", far_hits, remote_skeletons, preferred_element_type=jnp.float32
        ).astype(jnp.bfloat16)
        level_one = jnp.einsum(
            "kab,kbo->ao", couplings[0], chosen, preferred_element_type=jnp.float32
        )
        uplift = lax.dot_general(
            transfer[0], skeleton, (((0,), (0,)), ((), ())), preferred_element_type=jnp.float32
        )
        contrib = cluster_slots[:, None, None] * uplift[None]
        column_sums = lax.psum_scatter(contrib, "dev", scatter_dimension=2, tiled=True).astype(
            jnp.bfloat16
        )
        every_column = lax.all_gather(column_sums, "grp", axis=0, tiled=True)
        picked = every_column[far_clusters]
        partial_coupled = jnp.einsum(
            "ckab,ckbo->cao", cluster_couplings, picked, preferred_element_type=jnp.float32
        ).astype(jnp.bfloat16)
        whole_columns = lax.all_gather(partial_coupled, "dev", axis=2, tiled=True)
        coupled = whole_columns[local_cluster]
        downward = jnp.dot(transfer[0], coupled, preferred_element_type=jnp.float32)
        tree_rows = jnp.dot(
            leaf_basis,
            (level_one + downward).astype(jnp.bfloat16),
            preferred_element_type=jnp.float32,
        )
        far_part = jnp.zeros_like(tree_rows).at[ordering].set(tree_rows)
        return ridge_weight * direction + (near_sum + far_part)

    bottom_edge = ridge_weight + spectrum_gap
    top_edge = ridge_weight + spectrum_top
    centre = (top_edge + bottom_edge) / 2.0
    spread = (top_edge - bottom_edge) / 2.0
    sigma_ratio = centre / spread
    contraction = 1.0 / sigma_ratio
    direction = right_side / centre
    solution = direction
    residual = right_side
    for rounds in range(ITERS):
        residual = residual - operate(direction)
        rho_next = 1.0 / (2.0 * sigma_ratio - contraction)
        direction = rho_next * contraction * direction + 2.0 * rho_next / spread * residual
        solution = solution + direction
        contraction = rho_next
    return (solution, residual)


def fused_kernel(
    n,
    coords_ref,
    right_ref,
    perm_ref,
    near_ref,
    far_ref,
    coup_ref,
    transfer_ref,
    basis_ref,
    cluster_ref,
    farclus_ref,
    cluscoup_ref,
    ridge_ref,
    sol_ref,
    res_ref,
    points,
    wide,
    blocks,
    skel,
    moved,
    spread_t,
    chosen,
    mine,
    theirs,
    coup_out,
    coup_in,
    basis_p,
    basis_t,
    acc,
    direction,
    near_send,
    near_recv,
    tree_send,
    tree_recv,
    mate_send,
    mate_recv,
    grp_send,
    grp_recv,
):
    f32, bf16 = jnp.float32, jnp.bfloat16
    group = lax.axis_index("grp")
    me = lax.axis_index("dev")
    other = 1 - group
    chips = n // 2
    chip = lax.div(me, 2)
    core = lax.rem(me, 2)
    row = lax.rem(chip, 2)
    mate = chip * 2 + (1 - core)
    across = me + 2 - 4 * row
    leaf, outs = right_ref.shape
    rank = transfer_ref.shape[1]
    clusters = cluscoup_ref.shape[0]
    has_z = ((row == 0) & (me >= 4)) | ((row == 1) & (me + 4 < n))
    sends_z = ((row == 0) & (me + 4 < n)) | ((row == 1) & (me >= 4))
    z_target = jnp.where(sends_z, me + 4 - 8 * row, me)

    barrier = pltpu.get_barrier_semaphore()
    for step in range(1, n):
        pl.semaphore_signal(
            barrier, inc=1, device_id={"dev": lax.rem(me + step, n)}, device_id_type=MESH
        )
    pl.semaphore_signal(barrier, inc=1, device_id={"grp": other}, device_id_type=MESH)

    def near_copy(buf, stage, source, slot, target, size):
        return pltpu.make_async_remote_copy(
            src_ref=buf.at[pl.ds(source * size, size)],
            dst_ref=buf.at[pl.ds(slot * size, size)],
            send_sem=near_send.at[stage, slot],
            recv_sem=near_recv.at[stage, slot],
            device_id={"dev": target},
            device_id_type=MESH,
        )

    def near_start(buf, stage, size):
        near_copy(buf, stage, 0, 2, across, size).start()
        near_copy(buf, stage, 0, 1, mate, size).start()

        @pl.when(jnp.logical_not(has_z))
        def _():
            buf[pl.ds(3 * size, size), :] = jnp.zeros((size, buf.shape[1]), buf.dtype)

        @pl.when(jnp.logical_not(has_z) & (core == row))
        def _():
            buf[pl.ds(4 * size, size), :] = jnp.zeros((size, buf.shape[1]), buf.dtype)

    def near_relay(buf, stage, size):
        near_copy(buf, stage, 0, 2, across, size).wait_recv()

        @pl.when(sends_z)
        def _():
            near_copy(buf, stage, 2, 3, z_target, size).start()

        @pl.when(core == row)
        def _():
            near_copy(buf, stage, 2, 4, mate, size).start()

        @pl.when(has_z)
        def _():
            near_copy(buf, stage, 2, 3, mate, size).wait_recv()

        @pl.when(has_z & (core != row))
        def _():
            near_copy(buf, stage, 3, 4, mate, size).start()

    def near_finish(buf, stage, size):
        near_copy(buf, stage, 0, 1, mate, size).wait_recv()

        @pl.when(has_z | (core != row))
        def _():
            near_copy(buf, stage, 0, 4, mate, size).wait_recv()

    def near_drain(buf, stage, size):
        near_copy(buf, stage, 0, 1, mate, size).wait_send()
        near_copy(buf, stage, 0, 2, across, size).wait_send()

        @pl.when(sends_z)
        def _():
            near_copy(buf, stage, 2, 3, z_target, size).wait_send()

        @pl.when(has_z | (core == row))
        def _():
            near_copy(buf, stage, 0, 4, mate, size).wait_send()

    def tree_block(buf, owner, size):
        return buf.at[pl.ds(pl.multiple_of(owner * size, 16), size)]

    def tree_copy(buf, stage, step, owner, target, size, send, recv):
        return pltpu.make_async_remote_copy(
            src_ref=tree_block(buf, owner, size),
            dst_ref=tree_block(buf, owner, size),
            send_sem=send.at[stage, step],
            recv_sem=recv.at[stage, step],
            device_id={"dev": target},
            device_id_type=MESH,
        )

    def same_core(step):
        return lax.rem(chip + step + chips, chips) * 2 + core

    def tree_start(buf, stage, size):
        for step in range(1, chips):
            tree_copy(buf, stage, step, me, same_core(step), size, tree_send, tree_recv).start()
        tree_copy(buf, stage, 0, me, mate, size, mate_send, mate_recv).start()

    def tree_relay(buf, stage, size):
        for step in range(1, chips):
            owner = same_core(-step)
            tree_copy(buf, stage, step, owner, mate, size, tree_send, tree_recv).wait_recv()
            tree_copy(buf, stage, step, owner, mate, size, mate_send, mate_recv).start()

    def tree_finish(buf, stage, size):
        for step in range(chips):
            owner = lax.rem(chip - step + chips, chips) * 2 + (1 - core)
            tree_copy(buf, stage, step, owner, mate, size, mate_send, mate_recv).wait_recv()

    def tree_drain(buf, stage, size):
        for step in range(chips):
            tree_copy(buf, stage, step, me, mate, size, mate_send, mate_recv).wait_send()
            if step > 0:
                tree_copy(buf, stage, step, me, mate, size, tree_send, tree_recv).wait_send()

    def grp_copy(source, target, stage):
        return pltpu.make_async_remote_copy(
            src_ref=source,
            dst_ref=target,
            send_sem=grp_send.at[stage],
            recv_sem=grp_recv.at[stage],
            device_id={"grp": other},
            device_id_type=MESH,
        )

    points[pl.ds(0, leaf), :] = coords_ref[...]
    transfer_rows = transfer_ref[0]
    packed = rank + 16
    local_cluster = jnp.clip(cluster_ref[0] - group * clusters, 0, clusters - 1)
    lane_rows = lax.broadcasted_iota(jnp.int32, (16, rank), 0)
    tags = jnp.where(lane_rows == local_cluster, 1.0, 0.0).astype(bf16)
    own_rows = pl.multiple_of(me * packed, 16)
    moved[pl.ds(own_rows, rank), :] = transfer_rows.astype(f32).T.astype(bf16)
    moved[pl.ds(own_rows + rank, 16), :] = tags
    for place in range(clusters):
        total = jnp.zeros((rank, rank), f32)
        for k in range(farclus_ref.shape[1]):
            hit = (farclus_ref[local_cluster, k] == other * clusters + place).astype(f32)
            total = total + hit * cluscoup_ref[local_cluster, k].astype(f32)
        mine[:, place * rank : (place + 1) * rank] = total.astype(bf16)

    pl.semaphore_wait(barrier, n)
    near_start(points, 0, leaf)
    tree_start(moved, 0, packed)
    grp_copy(mine, theirs, 0).start()

    targets = lax.broadcasted_iota(jnp.int32, (leaf, leaf), 0)
    one_hot = jnp.where(targets == perm_ref[...], 1.0, 0.0).astype(bf16)
    placed = jnp.dot(one_hot, basis_ref[...], preferred_element_type=f32)
    basis_p[...] = placed.astype(bf16)
    basis_t[...] = placed.T.astype(bf16)
    for place in range(n):
        total = jnp.zeros((rank, rank), f32)
        for k in range(far_ref.shape[1]):
            hit = (far_ref[0, k] == group * n + place).astype(f32)
            total = total + hit * coup_ref[0, k].astype(f32)
        chosen[:, place * rank : (place + 1) * rank] = total.astype(bf16)

    last = (((1,), (1,)), ((), ()))
    left = coords_ref[...]
    left_sq = jnp.sum(left * left, axis=1, keepdims=True)

    def fill_block(slot, source):
        right = points[pl.ds(slot * leaf, leaf), :]
        right_sq = lax.dot_general(
            jnp.ones((8, right.shape[1]), f32),
            right * right,
            last,
            precision=lax.Precision.HIGHEST,
            preferred_element_type=f32,
        )[0:1, :]
        inner = lax.dot_general(
            left, right, last, precision=lax.Precision.HIGHEST, preferred_element_type=f32
        )
        block = jnp.exp(-kernel_scale * (left_sq + right_sq - 2.0 * inner))
        if source is not None:
            wanted = group * n + source
            hit = jnp.float32(0.0)
            for k in range(near_ref.shape[1]):
                listed = (near_ref[0, k] == wanted) & (near_ref[0, k] >= 0)
                hit = hit + listed.astype(f32)
            block = hit * block
        blocks[:, slot * leaf : (slot + 1) * leaf] = block.astype(bf16)

    ridge = ridge_ref[...]
    bottom_edge = ridge + spectrum_gap
    top_edge = ridge + spectrum_top
    centre = (top_edge + bottom_edge) / 2.0
    spread = (top_edge - bottom_edge) / 2.0
    sigma_ratio = centre / spread
    contraction = 1.0 / sigma_ratio
    start = right_ref[...] / centre
    direction[...] = start
    sol_ref[...] = start
    res_ref[...] = right_ref[...]

    def launch(rounds):
        values = direction[...].astype(bf16)
        wide[rounds, pl.ds(0, leaf), :] = values
        skeleton = jnp.dot(basis_t[...], values, preferred_element_type=f32).astype(bf16)
        skel[rounds, pl.ds(pl.multiple_of(me * rank, 16), rank), :] = skeleton
        tree_start(skel.at[rounds], rounds + 1, rank)
        near_start(wide.at[rounds], rounds + 1, leaf)

    fill_block(0, None)
    tree_relay(moved, 0, packed)
    near_relay(points, 0, leaf)
    launch(0)
    near_finish(points, 0, leaf)
    fill_block(1, mate)
    fill_block(2, across)
    tree_finish(moved, 0, packed)
    for place in range(n):
        part = moved[place * packed : place * packed + rank, :]
        for c in range(clusters):
            tag = moved[place * packed + rank : place * packed + packed, :][c : c + 1, :]
            spread_t[c * rank : (c + 1) * rank, place * rank : (place + 1) * rank] = (
                part.astype(f32) * tag.astype(f32)
            ).astype(bf16)

    for rounds in range(ITERS):
        stage = rounds + 1
        if rounds > 0:
            launch(rounds)
        acc[...] = ridge * direction[...] + jnp.dot(
            blocks[:, 0:leaf], wide[rounds, 0:leaf, :], preferred_element_type=f32
        )
        tree_relay(skel.at[rounds], stage, rank)
        near_relay(wide.at[rounds], stage, leaf)
        if rounds == 0:
            fill_block(3, me - 2 + 4 * row)
            fill_block(4, me - 1 + 2 * core)
            grp_copy(mine, theirs, 0).wait_recv()
        tree_finish(skel.at[rounds], stage, rank)
        sums = jnp.dot(spread_t[...], skel[rounds], preferred_element_type=f32).astype(bf16)
        coup_out[rounds] = jnp.dot(theirs[...], sums, preferred_element_type=f32).astype(bf16)
        grp_copy(coup_out.at[rounds], coup_in.at[rounds], stage).start()
        level_one = jnp.dot(chosen[...], skel[rounds], preferred_element_type=f32)
        near_finish(wide.at[rounds], stage, leaf)
        acc[...] += jnp.dot(
            blocks[:, leaf:], wide[rounds, leaf:, :], preferred_element_type=f32
        )
        grp_copy(coup_out.at[rounds], coup_in.at[rounds], stage).wait_recv()
        down = jnp.dot(transfer_rows, coup_in[rounds], preferred_element_type=f32)
        far_part = jnp.dot(
            basis_p[...], (level_one + down).astype(bf16), preferred_element_type=f32
        )
        residual = res_ref[...] - (acc[...] + far_part)
        res_ref[...] = residual
        rho_next = 1.0 / (2.0 * sigma_ratio - contraction)
        moved_on = rho_next * contraction * direction[...] + 2.0 * rho_next / spread * residual
        direction[...] = moved_on
        sol_ref[...] += moved_on
        contraction = rho_next

    near_drain(points, 0, leaf)
    tree_drain(moved, 0, packed)
    grp_copy(mine, theirs, 0).wait_send()
    for rounds in range(ITERS):
        near_drain(wide.at[rounds], rounds + 1, leaf)
        tree_drain(skel.at[rounds], rounds + 1, rank)
        grp_copy(coup_out.at[rounds], coup_in.at[rounds], rounds + 1).wait_send()


def fused_body(
    coords,
    right_side,
    leaf_perm,
    near_list,
    far_leaves,
    couplings,
    transfer,
    leaf_basis,
    cluster_of,
    far_clusters,
    cluster_couplings,
    ridge_weight,
):
    n = lax.axis_size("dev")
    leaf, dim = coords.shape
    outs = right_side.shape[1]
    rank = transfer.shape[1]
    clusters = cluster_couplings.shape[0]
    bf16, f32 = jnp.bfloat16, jnp.float32
    vmem = pl.BlockSpec(memory_space=pltpu.VMEM)
    smem = pl.BlockSpec(memory_space=pltpu.SMEM)
    sem = pltpu.SemaphoreType.DMA
    stages = ITERS + 1
    out = jax.ShapeDtypeStruct((leaf, outs), f32)
    return pl.pallas_call(
        functools.partial(fused_kernel, n),
        out_shape=(out, out),
        in_specs=[vmem, vmem, vmem, smem, smem, vmem, vmem, vmem, smem, smem, vmem, vmem],
        out_specs=(vmem, vmem),
        scratch_shapes=[
            pltpu.VMEM((5 * leaf, dim), f32),
            pltpu.VMEM((ITERS, 5 * leaf, outs), bf16),
            pltpu.VMEM((leaf, 5 * leaf), bf16),
            pltpu.VMEM((ITERS, n * rank, outs), bf16),
            pltpu.VMEM((n * (rank + 16), rank), bf16),
            pltpu.VMEM((clusters * rank, n * rank), bf16),
            pltpu.VMEM((rank, n * rank), bf16),
            pltpu.VMEM((rank, clusters * rank), bf16),
            pltpu.VMEM((rank, clusters * rank), bf16),
            pltpu.VMEM((ITERS, rank, outs), bf16),
            pltpu.VMEM((ITERS, rank, outs), bf16),
            pltpu.VMEM((leaf, rank), bf16),
            pltpu.VMEM((rank, leaf), bf16),
            pltpu.VMEM((leaf, outs), f32),
            pltpu.VMEM((leaf, outs), f32),
            sem((stages, 5)),
            sem((stages, 5)),
            sem((stages, n // 2)),
            sem((stages, n // 2)),
            sem((stages, n // 2)),
            sem((stages, n // 2)),
            sem((stages,)),
            sem((stages,)),
        ],
        compiler_params=pltpu.CompilerParams(
            collective_id=0, has_side_effects=True, vmem_limit_bytes=48 << 20
        ),
        name="fused_solve",
    )(
        coords,
        right_side,
        leaf_perm,
        near_list,
        far_leaves,
        couplings,
        transfer,
        leaf_basis,
        cluster_of,
        far_clusters,
        cluster_couplings,
        ridge_weight.reshape(1, 1),
    )


def solution(mesh):
    fits = mesh.shape["grp"] == 2 and mesh.shape["dev"] % 4 == 0
    placed = (
        P(("grp", "dev"), None),
        P(("grp", "dev"), None),
        P(("grp", "dev"), None),
        P(("grp", "dev"), None),
        P(("grp", "dev"), None),
        P(("grp", "dev"), None, None, None),
        P(("grp", "dev"), None, None),
        P(("grp", "dev"), None),
        P(("grp", "dev")),
        P("grp", None),
        P("grp", None, None, None),
        P(),
    )
    return jax.shard_map(
        fused_body if fits else body,
        mesh=mesh,
        in_specs=placed,
        out_specs=(P(("grp", "dev"), None), P(("grp", "dev"), None)),
        check_vma=False,
    )
```

```python
import functools

import jax
import jax.numpy as jnp
from jax import lax
from jax.experimental import pallas as pl
from jax.experimental.pallas import tpu as pltpu
from jax.sharding import PartitionSpec as P

MESH = pl.DeviceIdType.MESH
PARTS = 2

REACH = 2
FARREACH = 8
ITERS = 2


kernel_scale = 1.0 / 32.0
spectrum_gap = 0.5
spectrum_top = 8.0


def from_behind(shard, axis, by):
    devices = lax.axis_size(axis)
    pairs = [(i, i + by) for i in range(devices) if 0 <= i + by < devices]
    return lax.ppermute(shard, axis, pairs)


def kernel_block(left_points, right_points):
    inner_products = jnp.dot(
        left_points,
        right_points.T,
        precision=lax.Precision.HIGHEST,
        preferred_element_type=jnp.float32,
    )
    distance = (
        jnp.sum(left_points * left_points, axis=1)[:, None]
        + jnp.sum(right_points * right_points, axis=1)[None, :]
        - 2.0 * inner_products
    )
    return jnp.exp(-kernel_scale * distance).astype(jnp.bfloat16)


def body(
    coords,
    right_side,
    leaf_perm,
    near_list,
    far_leaves,
    couplings,
    transfer,
    leaf_basis,
    cluster_of,
    far_clusters,
    cluster_couplings,
    ridge_weight,
):
    dev_count = lax.axis_size("dev")
    group_index = lax.axis_index("grp")
    leaf_id = group_index * dev_count + lax.axis_index("dev")
    clusters_here = far_clusters.shape[0]
    local_cluster = cluster_of[0] - group_index * clusters_here
    ordering = leaf_perm[0]
    near_offsets = [offset for offset in range(-REACH, REACH + 1) if offset != 0]
    far_offsets = [offset for offset in range(-FARREACH, FARREACH + 1) if abs(offset) > REACH]
    neighbours = [from_behind(coords, "dev", -offset) for offset in near_offsets]
    near_flags = [
        jnp.any((near_list[0] == leaf_id + offset) & (near_list[0] >= 0)).astype(jnp.float32)
        for offset in near_offsets
    ]
    far_hits = jnp.stack(
        [far_leaves[0] == leaf_id + offset for offset in far_offsets], axis=1
    ).astype(jnp.bfloat16)
    own_block = kernel_block(coords, coords)
    near_blocks = [kernel_block(coords, neighbour_points) for neighbour_points in neighbours]
    cluster_slots = (jnp.arange(clusters_here) == local_cluster).astype(jnp.float32)

    def operate(direction):
        values = direction.astype(jnp.bfloat16)
        near_sum = jnp.dot(own_block, values, preferred_element_type=jnp.float32)
        for position in range(len(near_offsets)):
            remote = from_behind(values, "dev", -near_offsets[position])
            block_here = near_blocks[position]
            near_term = near_flags[position] * jnp.dot(
                block_here, remote, preferred_element_type=jnp.float32
            )
            near_sum = near_sum + near_term
        skeleton = lax.dot_general(
            leaf_basis,
            values[ordering],
            (((0,), (0,)), ((), ())),
            preferred_element_type=jnp.float32,
        ).astype(jnp.bfloat16)
        remote_skeletons = jnp.stack(
            [from_behind(skeleton, "dev", -offset) for offset in far_offsets]
        )
        chosen = jnp.einsum(
            "kj,jbo->kbo", far_hits, remote_skeletons, preferred_element_type=jnp.float32
        ).astype(jnp.bfloat16)
        level_one = jnp.einsum(
            "kab,kbo->ao", couplings[0], chosen, preferred_element_type=jnp.float32
        )
        uplift = lax.dot_general(
            transfer[0], skeleton, (((0,), (0,)), ((), ())), preferred_element_type=jnp.float32
        )
        contrib = cluster_slots[:, None, None] * uplift[None]
        column_sums = lax.psum_scatter(contrib, "dev", scatter_dimension=2, tiled=True).astype(
            jnp.bfloat16
        )
        every_column = lax.all_gather(column_sums, "grp", axis=0, tiled=True)
        picked = every_column[far_clusters]
        partial_coupled = jnp.einsum(
            "ckab,ckbo->cao", cluster_couplings, picked, preferred_element_type=jnp.float32
        ).astype(jnp.bfloat16)
        whole_columns = lax.all_gather(partial_coupled, "dev", axis=2, tiled=True)
        coupled = whole_columns[local_cluster]
        downward = jnp.dot(transfer[0], coupled, preferred_element_type=jnp.float32)
        tree_rows = jnp.dot(
            leaf_basis,
            (level_one + downward).astype(jnp.bfloat16),
            preferred_element_type=jnp.float32,
        )
        far_part = jnp.zeros_like(tree_rows).at[ordering].set(tree_rows)
        return ridge_weight * direction + (near_sum + far_part)

    bottom_edge = ridge_weight + spectrum_gap
    top_edge = ridge_weight + spectrum_top
    centre = (top_edge + bottom_edge) / 2.0
    spread = (top_edge - bottom_edge) / 2.0
    sigma_ratio = centre / spread
    contraction = 1.0 / sigma_ratio
    direction = right_side / centre
    solution = direction
    residual = right_side
    for rounds in range(ITERS):
        residual = residual - operate(direction)
        rho_next = 1.0 / (2.0 * sigma_ratio - contraction)
        direction = rho_next * contraction * direction + 2.0 * rho_next / spread * residual
        solution = solution + direction
        contraction = rho_next
    return (solution, residual)


def fused_kernel(
    n,
    coords_ref,
    right_ref,
    perm_ref,
    near_ref,
    far_ref,
    coup_ref,
    transfer_ref,
    basis_ref,
    cluster_ref,
    farclus_ref,
    cluscoup_ref,
    ridge_ref,
    sol_ref,
    res_ref,
    points,
    wide,
    blocks,
    skel,
    moved,
    spread_t,
    chosen,
    mine,
    theirs,
    coup_out,
    coup_in,
    basis_p,
    basis_t,
    acc,
    direction,
    near_send,
    near_recv,
    tree_send,
    tree_recv,
    mate_send,
    mate_recv,
    grp_send,
    grp_recv,
):
    f32, bf16 = jnp.float32, jnp.bfloat16
    group = lax.axis_index("grp")
    me = lax.axis_index("dev")
    other = 1 - group
    chips = n // 2
    chip = lax.div(me, 2)
    core = lax.rem(me, 2)
    row = lax.rem(chip, 2)
    mate = chip * 2 + (1 - core)
    across = me + 2 - 4 * row
    leaf, outs = right_ref.shape
    rank = transfer_ref.shape[1]
    clusters = cluscoup_ref.shape[0]
    has_z = ((row == 0) & (me >= 4)) | ((row == 1) & (me + 4 < n))
    sends_z = ((row == 0) & (me + 4 < n)) | ((row == 1) & (me >= 4))
    z_target = jnp.where(sends_z, me + 4 - 8 * row, me)

    barrier = pltpu.get_barrier_semaphore()
    for step in range(1, n):
        pl.semaphore_signal(
            barrier, inc=1, device_id={"dev": lax.rem(me + step, n)}, device_id_type=MESH
        )
    pl.semaphore_signal(barrier, inc=1, device_id={"grp": other}, device_id_type=MESH)

    def near_copy(buf, stage, source, slot, target, size, part):
        piece = size // PARTS
        return pltpu.make_async_remote_copy(
            src_ref=buf.at[pl.ds(source * size + part * piece, piece)],
            dst_ref=buf.at[pl.ds(slot * size + part * piece, piece)],
            send_sem=near_send.at[stage, slot, part],
            recv_sem=near_recv.at[stage, slot, part],
            device_id={"dev": target},
            device_id_type=MESH,
        )

    def near_start(buf, stage, size):
        for part in range(PARTS):
            near_copy(buf, stage, 0, 2, across, size, part).start()
        for part in range(PARTS):
            near_copy(buf, stage, 0, 1, mate, size, part).start()

        @pl.when(jnp.logical_not(has_z))
        def _():
            buf[pl.ds(3 * size, size), :] = jnp.zeros((size, buf.shape[1]), buf.dtype)

        @pl.when(jnp.logical_not(has_z) & (core == row))
        def _():
            buf[pl.ds(4 * size, size), :] = jnp.zeros((size, buf.shape[1]), buf.dtype)

    def near_relay(buf, stage, size):
        for part in range(PARTS):
            near_copy(buf, stage, 0, 2, across, size, part).wait_recv()

            @pl.when(sends_z)
            def _():
                near_copy(buf, stage, 2, 3, z_target, size, part).start()

            @pl.when(core == row)
            def _():
                near_copy(buf, stage, 2, 4, mate, size, part).start()

    def near_second(buf, stage, size):
        for part in range(PARTS):

            @pl.when(has_z)
            def _():
                near_copy(buf, stage, 2, 3, mate, size, part).wait_recv()

            @pl.when(has_z & (core != row))
            def _():
                near_copy(buf, stage, 3, 4, mate, size, part).start()

    def near_finish(buf, stage, size):
        for part in range(PARTS):
            near_copy(buf, stage, 0, 1, mate, size, part).wait_recv()

            @pl.when(has_z | (core != row))
            def _():
                near_copy(buf, stage, 0, 4, mate, size, part).wait_recv()

    def near_drain(buf, stage, size):
        for part in range(PARTS):
            near_copy(buf, stage, 0, 1, mate, size, part).wait_send()
            near_copy(buf, stage, 0, 2, across, size, part).wait_send()

            @pl.when(sends_z)
            def _():
                near_copy(buf, stage, 2, 3, z_target, size, part).wait_send()

            @pl.when(has_z | (core == row))
            def _():
                near_copy(buf, stage, 0, 4, mate, size, part).wait_send()

    def tree_block(buf, owner, size):
        return buf.at[pl.ds(pl.multiple_of(owner * size, 16), size)]

    def tree_copy(buf, stage, step, owner, target, size, send, recv):
        return pltpu.make_async_remote_copy(
            src_ref=tree_block(buf, owner, size),
            dst_ref=tree_block(buf, owner, size),
            send_sem=send.at[stage, step],
            recv_sem=recv.at[stage, step],
            device_id={"dev": target},
            device_id_type=MESH,
        )

    def same_core(step):
        return lax.rem(chip + step + chips, chips) * 2 + core

    def tree_start(buf, stage, size):
        for step in range(1, chips):
            tree_copy(buf, stage, step, me, same_core(step), size, tree_send, tree_recv).start()
        tree_copy(buf, stage, 0, me, mate, size, mate_send, mate_recv).start()

    def tree_relay(buf, stage, size):
        for step in range(1, chips):
            owner = same_core(-step)
            tree_copy(buf, stage, step, owner, mate, size, tree_send, tree_recv).wait_recv()
            tree_copy(buf, stage, step, owner, mate, size, mate_send, mate_recv).start()

    def tree_finish(buf, stage, size):
        for step in range(chips):
            owner = lax.rem(chip - step + chips, chips) * 2 + (1 - core)
            tree_copy(buf, stage, step, owner, mate, size, mate_send, mate_recv).wait_recv()

    def tree_drain(buf, stage, size):
        for step in range(chips):
            tree_copy(buf, stage, step, me, mate, size, mate_send, mate_recv).wait_send()
            if step > 0:
                tree_copy(buf, stage, step, me, mate, size, tree_send, tree_recv).wait_send()

    def grp_copy(source, target, stage):
        return pltpu.make_async_remote_copy(
            src_ref=source,
            dst_ref=target,
            send_sem=grp_send.at[stage],
            recv_sem=grp_recv.at[stage],
            device_id={"grp": other},
            device_id_type=MESH,
        )

    dim = coords_ref.shape[0]
    points[pl.ds(0, dim), :] = coords_ref[...]
    transfer_rows = transfer_ref[0]
    packed = rank + 16
    local_cluster = jnp.clip(cluster_ref[0] - group * clusters, 0, clusters - 1)
    lane_rows = lax.broadcasted_iota(jnp.int32, (16, rank), 0)
    tags = jnp.where(lane_rows == local_cluster, 1.0, 0.0).astype(bf16)
    own_rows = pl.multiple_of(me * packed, 16)
    moved[pl.ds(own_rows, rank), :] = transfer_rows.astype(f32).T.astype(bf16)
    moved[pl.ds(own_rows + rank, 16), :] = tags
    for place in range(clusters):
        total = jnp.zeros((rank, rank), f32)
        for k in range(farclus_ref.shape[1]):
            hit = (farclus_ref[local_cluster, k] == other * clusters + place).astype(f32)
            total = total + hit * cluscoup_ref[local_cluster, k].astype(f32)
        mine[:, place * rank : (place + 1) * rank] = total.astype(bf16)

    targets = lax.broadcasted_iota(jnp.int32, (leaf, leaf), 0)
    one_hot = jnp.where(targets == perm_ref[...], 1.0, 0.0).astype(bf16)
    placed = jnp.dot(one_hot, basis_ref[...], preferred_element_type=f32)
    basis_p[...] = placed.astype(bf16)
    basis_t[...] = placed.T.astype(bf16)
    ridge = ridge_ref[...]
    bottom_edge = ridge + spectrum_gap
    top_edge = ridge + spectrum_top
    centre = (top_edge + bottom_edge) / 2.0
    spread = (top_edge - bottom_edge) / 2.0
    sigma_ratio = centre / spread
    contraction = 1.0 / sigma_ratio
    start = right_ref[...] / centre
    direction[...] = start
    sol_ref[...] = start
    res_ref[...] = right_ref[...]

    def launch(rounds):
        values = direction[...].astype(bf16)
        wide[rounds, pl.ds(0, leaf), :] = values
        skeleton = jnp.dot(basis_t[...], values, preferred_element_type=f32).astype(bf16)
        skel[rounds, pl.ds(pl.multiple_of(me * rank, 16), rank), :] = skeleton
        tree_start(skel.at[rounds], rounds + 1, rank)
        near_start(wide.at[rounds], rounds + 1, leaf)

    pl.semaphore_wait(barrier, n)
    near_start(points, 0, dim)
    launch(0)
    tree_start(moved, 0, packed)
    grp_copy(mine, theirs, 0).start()

    for place in range(n):
        total = jnp.zeros((rank, rank), f32)
        for k in range(far_ref.shape[1]):
            hit = (far_ref[0, k] == group * n + place).astype(f32)
            total = total + hit * coup_ref[0, k].astype(f32)
        chosen[:, place * rank : (place + 1) * rank] = total.astype(bf16)

    left = coords_ref[...].T
    left_sq = jnp.sum(left * left, axis=1, keepdims=True)

    def fill_block(slot, source):
        right = points[pl.ds(slot * dim, dim), :]
        right_sq = jnp.sum(right * right, axis=0, keepdims=True)
        inner = jnp.dot(
            left, right, precision=lax.Precision.HIGHEST, preferred_element_type=f32
        )
        block = jnp.exp(-kernel_scale * (left_sq + right_sq - 2.0 * inner))
        if source is not None:
            wanted = group * n + source
            hit = jnp.float32(0.0)
            for k in range(near_ref.shape[1]):
                listed = (near_ref[0, k] == wanted) & (near_ref[0, k] >= 0)
                hit = hit + listed.astype(f32)
            block = hit * block
        blocks[:, slot * leaf : (slot + 1) * leaf] = block.astype(bf16)

    def spread_transfers():
        for place in range(n):
            part = moved[place * packed : place * packed + rank, :]
            for c in range(clusters):
                tag = moved[place * packed + rank : place * packed + packed, :][c : c + 1, :]
                spread_t[c * rank : (c + 1) * rank, place * rank : (place + 1) * rank] = (
                    part.astype(f32) * tag.astype(f32)
                ).astype(bf16)

    for rounds in range(ITERS):
        stage = rounds + 1
        if rounds > 0:
            launch(rounds)
        if rounds == 0:
            fill_block(0, None)
            near_relay(points, 0, dim)
            tree_relay(moved, 0, packed)
            near_second(points, 0, dim)
        acc[...] = ridge * direction[...] + jnp.dot(
            blocks[:, 0:leaf], wide[rounds, 0:leaf, :], preferred_element_type=f32
        )
        tree_relay(skel.at[rounds], stage, rank)
        near_relay(wide.at[rounds], stage, leaf)
        if rounds == 0:
            near_finish(points, 0, dim)
            fill_block(1, mate)
            fill_block(2, across)
            near_second(wide.at[rounds], stage, leaf)
            tree_finish(moved, 0, packed)
            spread_transfers()
            grp_copy(mine, theirs, 0).wait_recv()
        else:
            near_second(wide.at[rounds], stage, leaf)
        tree_finish(skel.at[rounds], stage, rank)
        sums = jnp.dot(spread_t[...], skel[rounds], preferred_element_type=f32).astype(bf16)
        coup_out[rounds] = jnp.dot(theirs[...], sums, preferred_element_type=f32).astype(bf16)
        grp_copy(coup_out.at[rounds], coup_in.at[rounds], stage).start()
        level_one = jnp.dot(chosen[...], skel[rounds], preferred_element_type=f32)
        if rounds == 0:
            fill_block(3, me - 2 + 4 * row)
            fill_block(4, me - 1 + 2 * core)
        near_finish(wide.at[rounds], stage, leaf)
        acc[...] += jnp.dot(
            blocks[:, leaf:], wide[rounds, leaf:, :], preferred_element_type=f32
        )
        grp_copy(coup_out.at[rounds], coup_in.at[rounds], stage).wait_recv()
        down = jnp.dot(transfer_rows, coup_in[rounds], preferred_element_type=f32)
        far_part = jnp.dot(
            basis_p[...], (level_one + down).astype(bf16), preferred_element_type=f32
        )
        residual = res_ref[...] - (acc[...] + far_part)
        res_ref[...] = residual
        rho_next = 1.0 / (2.0 * sigma_ratio - contraction)
        moved_on = rho_next * contraction * direction[...] + 2.0 * rho_next / spread * residual
        direction[...] = moved_on
        sol_ref[...] += moved_on
        contraction = rho_next

    near_drain(points, 0, dim)
    tree_drain(moved, 0, packed)
    grp_copy(mine, theirs, 0).wait_send()
    for rounds in range(ITERS):
        near_drain(wide.at[rounds], rounds + 1, leaf)
        tree_drain(skel.at[rounds], rounds + 1, rank)
        grp_copy(coup_out.at[rounds], coup_in.at[rounds], rounds + 1).wait_send()


def fused_body(
    coords,
    right_side,
    leaf_perm,
    near_list,
    far_leaves,
    couplings,
    transfer,
    leaf_basis,
    cluster_of,
    far_clusters,
    cluster_couplings,
    ridge_weight,
):
    n = lax.axis_size("dev")
    leaf, dim = coords.shape
    outs = right_side.shape[1]
    rank = transfer.shape[1]
    clusters = cluster_couplings.shape[0]
    bf16, f32 = jnp.bfloat16, jnp.float32
    vmem = pl.BlockSpec(memory_space=pltpu.VMEM)
    smem = pl.BlockSpec(memory_space=pltpu.SMEM)
    sem = pltpu.SemaphoreType.DMA
    stages = ITERS + 1
    out = jax.ShapeDtypeStruct((leaf, outs), f32)
    return pl.pallas_call(
        functools.partial(fused_kernel, n),
        out_shape=(out, out),
        in_specs=[vmem, vmem, vmem, smem, smem, vmem, vmem, vmem, smem, smem, vmem, vmem],
        out_specs=(vmem, vmem),
        scratch_shapes=[
            pltpu.VMEM((5 * dim, leaf), f32),
            pltpu.VMEM((ITERS, 5 * leaf, outs), bf16),
            pltpu.VMEM((leaf, 5 * leaf), bf16),
            pltpu.VMEM((ITERS, n * rank, outs), bf16),
            pltpu.VMEM((n * (rank + 16), rank), bf16),
            pltpu.VMEM((clusters * rank, n * rank), bf16),
            pltpu.VMEM((rank, n * rank), bf16),
            pltpu.VMEM((rank, clusters * rank), bf16),
            pltpu.VMEM((rank, clusters * rank), bf16),
            pltpu.VMEM((ITERS, rank, outs), bf16),
            pltpu.VMEM((ITERS, rank, outs), bf16),
            pltpu.VMEM((leaf, rank), bf16),
            pltpu.VMEM((rank, leaf), bf16),
            pltpu.VMEM((leaf, outs), f32),
            pltpu.VMEM((leaf, outs), f32),
            sem((stages, 5, PARTS)),
            sem((stages, 5, PARTS)),
            sem((stages, n // 2)),
            sem((stages, n // 2)),
            sem((stages, n // 2)),
            sem((stages, n // 2)),
            sem((stages,)),
            sem((stages,)),
        ],
        compiler_params=pltpu.CompilerParams(
            collective_id=0, has_side_effects=True, vmem_limit_bytes=48 << 20
        ),
        name="fused_solve",
    )(
        coords.T,
        right_side,
        leaf_perm,
        near_list,
        far_leaves,
        couplings,
        transfer,
        leaf_basis,
        cluster_of,
        far_clusters,
        cluster_couplings,
        ridge_weight.reshape(1, 1),
    )


def solution(mesh):
    fits = mesh.shape["grp"] == 2 and mesh.shape["dev"] % 4 == 0
    placed = (
        P(("grp", "dev"), None),
        P(("grp", "dev"), None),
        P(("grp", "dev"), None),
        P(("grp", "dev"), None),
        P(("grp", "dev"), None),
        P(("grp", "dev"), None, None, None),
        P(("grp", "dev"), None, None),
        P(("grp", "dev"), None),
        P(("grp", "dev")),
        P("grp", None),
        P("grp", None, None, None),
        P(),
    )
    return jax.shard_map(
        fused_body if fits else body,
        mesh=mesh,
        in_specs=placed,
        out_specs=(P(("grp", "dev"), None), P(("grp", "dev"), None)),
        check_vma=False,
    )
```

```python
import functools

import jax
import jax.numpy as jnp
from jax import lax
from jax.experimental import pallas as pl
from jax.experimental.pallas import tpu as pltpu
from jax.sharding import PartitionSpec as P

MESH = pl.DeviceIdType.MESH
PARTS = 2

REACH = 2
FARREACH = 8
ITERS = 2


kernel_scale = 1.0 / 32.0
spectrum_gap = 0.5
spectrum_top = 8.0


def from_behind(shard, axis, by):
    devices = lax.axis_size(axis)
    pairs = [(i, i + by) for i in range(devices) if 0 <= i + by < devices]
    return lax.ppermute(shard, axis, pairs)


def kernel_block(left_points, right_points):
    inner_products = jnp.dot(
        left_points,
        right_points.T,
        precision=lax.Precision.HIGHEST,
        preferred_element_type=jnp.float32,
    )
    distance = (
        jnp.sum(left_points * left_points, axis=1)[:, None]
        + jnp.sum(right_points * right_points, axis=1)[None, :]
        - 2.0 * inner_products
    )
    return jnp.exp(-kernel_scale * distance).astype(jnp.bfloat16)


def body(
    coords,
    right_side,
    leaf_perm,
    near_list,
    far_leaves,
    couplings,
    transfer,
    leaf_basis,
    cluster_of,
    far_clusters,
    cluster_couplings,
    ridge_weight,
):
    dev_count = lax.axis_size("dev")
    group_index = lax.axis_index("grp")
    leaf_id = group_index * dev_count + lax.axis_index("dev")
    clusters_here = far_clusters.shape[0]
    local_cluster = cluster_of[0] - group_index * clusters_here
    ordering = leaf_perm[0]
    near_offsets = [offset for offset in range(-REACH, REACH + 1) if offset != 0]
    far_offsets = [offset for offset in range(-FARREACH, FARREACH + 1) if abs(offset) > REACH]
    neighbours = [from_behind(coords, "dev", -offset) for offset in near_offsets]
    near_flags = [
        jnp.any((near_list[0] == leaf_id + offset) & (near_list[0] >= 0)).astype(jnp.float32)
        for offset in near_offsets
    ]
    far_hits = jnp.stack(
        [far_leaves[0] == leaf_id + offset for offset in far_offsets], axis=1
    ).astype(jnp.bfloat16)
    own_block = kernel_block(coords, coords)
    near_blocks = [kernel_block(coords, neighbour_points) for neighbour_points in neighbours]
    cluster_slots = (jnp.arange(clusters_here) == local_cluster).astype(jnp.float32)

    def operate(direction):
        values = direction.astype(jnp.bfloat16)
        near_sum = jnp.dot(own_block, values, preferred_element_type=jnp.float32)
        for position in range(len(near_offsets)):
            remote = from_behind(values, "dev", -near_offsets[position])
            block_here = near_blocks[position]
            near_term = near_flags[position] * jnp.dot(
                block_here, remote, preferred_element_type=jnp.float32
            )
            near_sum = near_sum + near_term
        skeleton = lax.dot_general(
            leaf_basis,
            values[ordering],
            (((0,), (0,)), ((), ())),
            preferred_element_type=jnp.float32,
        ).astype(jnp.bfloat16)
        remote_skeletons = jnp.stack(
            [from_behind(skeleton, "dev", -offset) for offset in far_offsets]
        )
        chosen = jnp.einsum(
            "kj,jbo->kbo", far_hits, remote_skeletons, preferred_element_type=jnp.float32
        ).astype(jnp.bfloat16)
        level_one = jnp.einsum(
            "kab,kbo->ao", couplings[0], chosen, preferred_element_type=jnp.float32
        )
        uplift = lax.dot_general(
            transfer[0], skeleton, (((0,), (0,)), ((), ())), preferred_element_type=jnp.float32
        )
        contrib = cluster_slots[:, None, None] * uplift[None]
        column_sums = lax.psum_scatter(contrib, "dev", scatter_dimension=2, tiled=True).astype(
            jnp.bfloat16
        )
        every_column = lax.all_gather(column_sums, "grp", axis=0, tiled=True)
        picked = every_column[far_clusters]
        partial_coupled = jnp.einsum(
            "ckab,ckbo->cao", cluster_couplings, picked, preferred_element_type=jnp.float32
        ).astype(jnp.bfloat16)
        whole_columns = lax.all_gather(partial_coupled, "dev", axis=2, tiled=True)
        coupled = whole_columns[local_cluster]
        downward = jnp.dot(transfer[0], coupled, preferred_element_type=jnp.float32)
        tree_rows = jnp.dot(
            leaf_basis,
            (level_one + downward).astype(jnp.bfloat16),
            preferred_element_type=jnp.float32,
        )
        far_part = jnp.zeros_like(tree_rows).at[ordering].set(tree_rows)
        return ridge_weight * direction + (near_sum + far_part)

    bottom_edge = ridge_weight + spectrum_gap
    top_edge = ridge_weight + spectrum_top
    centre = (top_edge + bottom_edge) / 2.0
    spread = (top_edge - bottom_edge) / 2.0
    sigma_ratio = centre / spread
    contraction = 1.0 / sigma_ratio
    direction = right_side / centre
    solution = direction
    residual = right_side
    for rounds in range(ITERS):
        residual = residual - operate(direction)
        rho_next = 1.0 / (2.0 * sigma_ratio - contraction)
        direction = rho_next * contraction * direction + 2.0 * rho_next / spread * residual
        solution = solution + direction
        contraction = rho_next
    return (solution, residual)


def fused_kernel(
    n,
    coords_ref,
    right_ref,
    perm_ref,
    near_ref,
    far_ref,
    coup_ref,
    transfer_ref,
    basis_ref,
    cluster_ref,
    farclus_ref,
    cluscoup_ref,
    ridge_ref,
    sol_ref,
    res_ref,
    points,
    wide,
    blocks,
    skel,
    moved,
    spread_t,
    chosen,
    mine,
    theirs,
    coup_out,
    coup_in,
    basis_p,
    basis_t,
    acc,
    direction,
    near_send,
    near_recv,
    tree_send,
    tree_recv,
    mate_send,
    mate_recv,
    grp_send,
    grp_recv,
):
    f32, bf16 = jnp.float32, jnp.bfloat16
    group = lax.axis_index("grp")
    me = lax.axis_index("dev")
    other = 1 - group
    chips = n // 2
    chip = lax.div(me, 2)
    core = lax.rem(me, 2)
    row = lax.rem(chip, 2)
    mate = chip * 2 + (1 - core)
    across = me + 2 - 4 * row
    leaf, outs = right_ref.shape
    rank = transfer_ref.shape[1]
    clusters = cluscoup_ref.shape[0]
    has_z = ((row == 0) & (me >= 4)) | ((row == 1) & (me + 4 < n))
    sends_z = ((row == 0) & (me + 4 < n)) | ((row == 1) & (me >= 4))
    z_target = jnp.where(sends_z, me + 4 - 8 * row, me)

    barrier = pltpu.get_barrier_semaphore()
    for step in range(1, n):
        pl.semaphore_signal(
            barrier, inc=1, device_id={"dev": lax.rem(me + step, n)}, device_id_type=MESH
        )
    pl.semaphore_signal(barrier, inc=1, device_id={"grp": other}, device_id_type=MESH)

    def near_copy(buf, stage, source, slot, target, size, part):
        piece = size // PARTS
        return pltpu.make_async_remote_copy(
            src_ref=buf.at[pl.ds(source * size + part * piece, piece)],
            dst_ref=buf.at[pl.ds(slot * size + part * piece, piece)],
            send_sem=near_send.at[stage, slot, part],
            recv_sem=near_recv.at[stage, slot, part],
            device_id={"dev": target},
            device_id_type=MESH,
        )

    def near_start(buf, stage, size):
        for part in range(PARTS):
            near_copy(buf, stage, 0, 2, across, size, part).start()
        for part in range(PARTS):
            near_copy(buf, stage, 0, 1, mate, size, part).start()

        @pl.when(jnp.logical_not(has_z))
        def _():
            buf[pl.ds(3 * size, size), :] = jnp.zeros((size, buf.shape[1]), buf.dtype)

        @pl.when(jnp.logical_not(has_z) & (core == row))
        def _():
            buf[pl.ds(4 * size, size), :] = jnp.zeros((size, buf.shape[1]), buf.dtype)

    def near_relay(buf, stage, size):
        for part in range(PARTS):
            near_copy(buf, stage, 0, 2, across, size, part).wait_recv()

            @pl.when(sends_z)
            def _():
                near_copy(buf, stage, 2, 3, z_target, size, part).start()

            @pl.when(core == row)
            def _():
                near_copy(buf, stage, 2, 4, mate, size, part).start()

    def near_second(buf, stage, size):
        for part in range(PARTS):

            @pl.when(has_z)
            def _():
                near_copy(buf, stage, 2, 3, mate, size, part).wait_recv()

            @pl.when(has_z & (core != row))
            def _():
                near_copy(buf, stage, 3, 4, mate, size, part).start()

    def near_finish(buf, stage, size):
        for part in range(PARTS):
            near_copy(buf, stage, 0, 1, mate, size, part).wait_recv()

            @pl.when(has_z | (core != row))
            def _():
                near_copy(buf, stage, 0, 4, mate, size, part).wait_recv()

    def near_drain(buf, stage, size):
        for part in range(PARTS):
            near_copy(buf, stage, 0, 1, mate, size, part).wait_send()
            near_copy(buf, stage, 0, 2, across, size, part).wait_send()

            @pl.when(sends_z)
            def _():
                near_copy(buf, stage, 2, 3, z_target, size, part).wait_send()

            @pl.when(has_z | (core == row))
            def _():
                near_copy(buf, stage, 0, 4, mate, size, part).wait_send()

    def tree_block(buf, owner, size):
        return buf.at[pl.ds(pl.multiple_of(owner * size, 16), size)]

    def tree_copy(buf, stage, step, owner, target, size, send, recv):
        return pltpu.make_async_remote_copy(
            src_ref=tree_block(buf, owner, size),
            dst_ref=tree_block(buf, owner, size),
            send_sem=send.at[stage, step],
            recv_sem=recv.at[stage, step],
            device_id={"dev": target},
            device_id_type=MESH,
        )

    planes = chips // 2
    plane = lax.div(chip, 2)

    def along(step):
        return (lax.rem(plane + step % planes, planes) * 2 + row) * 2 + core

    def owner_of(step, side):
        flipped = row if step < planes else 1 - row
        return (lax.rem(plane - step % planes + planes, planes) * 2 + flipped) * 2 + side

    def tree_start(buf, stage, size):
        tree_copy(buf, stage, planes, me, across, size, tree_send, tree_recv).start()
        for step in range(1, planes):
            tree_copy(buf, stage, step, me, along(step), size, tree_send, tree_recv).start()
        tree_copy(buf, stage, 0, me, mate, size, mate_send, mate_recv).start()

    def tree_pass(buf, stage, step, size):
        owner = owner_of(step, core)
        tree_copy(buf, stage, step, owner, mate, size, mate_send, mate_recv).start()

    def tree_relay(buf, stage, size):
        for step in (planes, *range(1, planes), *range(planes + 1, chips)):
            owner = owner_of(step, core)
            tree_copy(buf, stage, step, owner, mate, size, tree_send, tree_recv).wait_recv()
            if step == planes:
                for later in range(planes + 1, chips):
                    tree_copy(
                        buf, stage, later, across, along(later), size, tree_send, tree_recv
                    ).start()
            tree_pass(buf, stage, step, size)

    def tree_finish(buf, stage, size):
        for step in range(chips):
            owner = owner_of(step, 1 - core)
            tree_copy(buf, stage, step, owner, mate, size, mate_send, mate_recv).wait_recv()

    def tree_drain(buf, stage, size):
        for step in range(chips):
            tree_copy(buf, stage, step, me, mate, size, mate_send, mate_recv).wait_send()
            if step > 0:
                tree_copy(buf, stage, step, me, mate, size, tree_send, tree_recv).wait_send()

    def grp_copy(source, target, stage):
        return pltpu.make_async_remote_copy(
            src_ref=source,
            dst_ref=target,
            send_sem=grp_send.at[stage],
            recv_sem=grp_recv.at[stage],
            device_id={"grp": other},
            device_id_type=MESH,
        )

    dim = coords_ref.shape[0]
    points[pl.ds(0, dim), :] = coords_ref[...]
    transfer_rows = transfer_ref[0]
    packed = rank + 16
    local_cluster = jnp.clip(cluster_ref[0] - group * clusters, 0, clusters - 1)
    lane_rows = lax.broadcasted_iota(jnp.int32, (16, rank), 0)
    tags = jnp.where(lane_rows == local_cluster, 1.0, 0.0).astype(bf16)
    own_rows = pl.multiple_of(me * packed, 16)
    moved[pl.ds(own_rows, rank), :] = transfer_rows.astype(f32).T.astype(bf16)
    moved[pl.ds(own_rows + rank, 16), :] = tags
    for place in range(clusters):
        total = jnp.zeros((rank, rank), f32)
        for k in range(farclus_ref.shape[1]):
            hit = (farclus_ref[local_cluster, k] == other * clusters + place).astype(f32)
            total = total + hit * cluscoup_ref[local_cluster, k].astype(f32)
        mine[:, place * rank : (place + 1) * rank] = total.astype(bf16)

    targets = lax.broadcasted_iota(jnp.int32, (leaf, leaf), 0)
    one_hot = jnp.where(targets == perm_ref[...], 1.0, 0.0).astype(bf16)
    placed = jnp.dot(one_hot, basis_ref[...], preferred_element_type=f32)
    basis_p[...] = placed.astype(bf16)
    basis_t[...] = placed.T.astype(bf16)
    ridge = ridge_ref[...]
    bottom_edge = ridge + spectrum_gap
    top_edge = ridge + spectrum_top
    centre = (top_edge + bottom_edge) / 2.0
    spread = (top_edge - bottom_edge) / 2.0
    sigma_ratio = centre / spread
    contraction = 1.0 / sigma_ratio
    start = right_ref[...] / centre
    direction[...] = start
    sol_ref[...] = start
    res_ref[...] = right_ref[...]

    def launch(rounds):
        values = direction[...].astype(bf16)
        wide[rounds, pl.ds(0, leaf), :] = values
        skeleton = jnp.dot(basis_t[...], values, preferred_element_type=f32).astype(bf16)
        skel[rounds, pl.ds(pl.multiple_of(me * rank, 16), rank), :] = skeleton
        tree_start(skel.at[rounds], rounds + 1, rank)
        near_start(wide.at[rounds], rounds + 1, leaf)

    pl.semaphore_wait(barrier, n)
    near_start(points, 0, dim)
    launch(0)
    tree_start(moved, 0, packed)
    grp_copy(mine, theirs, 0).start()

    for place in range(n):
        total = jnp.zeros((rank, rank), f32)
        for k in range(far_ref.shape[1]):
            hit = (far_ref[0, k] == group * n + place).astype(f32)
            total = total + hit * coup_ref[0, k].astype(f32)
        chosen[:, place * rank : (place + 1) * rank] = total.astype(bf16)

    left = coords_ref[...].T
    left_sq = jnp.sum(left * left, axis=1, keepdims=True)

    def fill_block(slot, source):
        right = points[pl.ds(slot * dim, dim), :]
        right_sq = jnp.sum(right * right, axis=0, keepdims=True)
        inner = jnp.dot(
            left, right, precision=lax.Precision.HIGHEST, preferred_element_type=f32
        )
        block = jnp.exp(-kernel_scale * (left_sq + right_sq - 2.0 * inner))
        if source is not None:
            wanted = group * n + source
            hit = jnp.float32(0.0)
            for k in range(near_ref.shape[1]):
                listed = (near_ref[0, k] == wanted) & (near_ref[0, k] >= 0)
                hit = hit + listed.astype(f32)
            block = hit * block
        blocks[:, slot * leaf : (slot + 1) * leaf] = block.astype(bf16)

    def spread_transfers():
        for place in range(n):
            part = moved[place * packed : place * packed + rank, :]
            for c in range(clusters):
                tag = moved[place * packed + rank : place * packed + packed, :][c : c + 1, :]
                spread_t[c * rank : (c + 1) * rank, place * rank : (place + 1) * rank] = (
                    part.astype(f32) * tag.astype(f32)
                ).astype(bf16)

    for rounds in range(ITERS):
        stage = rounds + 1
        if rounds > 0:
            launch(rounds)
        if rounds == 0:
            fill_block(0, None)
            near_relay(points, 0, dim)
            tree_relay(moved, 0, packed)
            near_second(points, 0, dim)
        acc[...] = ridge * direction[...] + jnp.dot(
            blocks[:, 0:leaf], wide[rounds, 0:leaf, :], preferred_element_type=f32
        )
        tree_relay(skel.at[rounds], stage, rank)
        near_relay(wide.at[rounds], stage, leaf)
        if rounds == 0:
            near_finish(points, 0, dim)
            fill_block(1, mate)
            fill_block(2, across)
            near_second(wide.at[rounds], stage, leaf)
            tree_finish(moved, 0, packed)
            spread_transfers()
            grp_copy(mine, theirs, 0).wait_recv()
        else:
            near_second(wide.at[rounds], stage, leaf)
        tree_finish(skel.at[rounds], stage, rank)
        sums = jnp.dot(spread_t[...], skel[rounds], preferred_element_type=f32).astype(bf16)
        coup_out[rounds] = jnp.dot(theirs[...], sums, preferred_element_type=f32).astype(bf16)
        grp_copy(coup_out.at[rounds], coup_in.at[rounds], stage).start()
        level_one = jnp.dot(chosen[...], skel[rounds], preferred_element_type=f32)
        if rounds == 0:
            fill_block(3, me - 2 + 4 * row)
            fill_block(4, me - 1 + 2 * core)
        near_finish(wide.at[rounds], stage, leaf)
        acc[...] += jnp.dot(
            blocks[:, leaf:], wide[rounds, leaf:, :], preferred_element_type=f32
        )
        grp_copy(coup_out.at[rounds], coup_in.at[rounds], stage).wait_recv()
        down = jnp.dot(transfer_rows, coup_in[rounds], preferred_element_type=f32)
        far_part = jnp.dot(
            basis_p[...], (level_one + down).astype(bf16), preferred_element_type=f32
        )
        residual = res_ref[...] - (acc[...] + far_part)
        res_ref[...] = residual
        rho_next = 1.0 / (2.0 * sigma_ratio - contraction)
        moved_on = rho_next * contraction * direction[...] + 2.0 * rho_next / spread * residual
        direction[...] = moved_on
        sol_ref[...] += moved_on
        contraction = rho_next

    near_drain(points, 0, dim)
    tree_drain(moved, 0, packed)
    grp_copy(mine, theirs, 0).wait_send()
    for rounds in range(ITERS):
        near_drain(wide.at[rounds], rounds + 1, leaf)
        tree_drain(skel.at[rounds], rounds + 1, rank)
        grp_copy(coup_out.at[rounds], coup_in.at[rounds], rounds + 1).wait_send()


def fused_body(
    coords,
    right_side,
    leaf_perm,
    near_list,
    far_leaves,
    couplings,
    transfer,
    leaf_basis,
    cluster_of,
    far_clusters,
    cluster_couplings,
    ridge_weight,
):
    n = lax.axis_size("dev")
    leaf, dim = coords.shape
    outs = right_side.shape[1]
    rank = transfer.shape[1]
    clusters = cluster_couplings.shape[0]
    bf16, f32 = jnp.bfloat16, jnp.float32
    vmem = pl.BlockSpec(memory_space=pltpu.VMEM)
    smem = pl.BlockSpec(memory_space=pltpu.SMEM)
    sem = pltpu.SemaphoreType.DMA
    stages = ITERS + 1
    out = jax.ShapeDtypeStruct((leaf, outs), f32)
    return pl.pallas_call(
        functools.partial(fused_kernel, n),
        out_shape=(out, out),
        in_specs=[vmem, vmem, vmem, smem, smem, vmem, vmem, vmem, smem, smem, vmem, vmem],
        out_specs=(vmem, vmem),
        scratch_shapes=[
            pltpu.VMEM((5 * dim, leaf), f32),
            pltpu.VMEM((ITERS, 5 * leaf, outs), bf16),
            pltpu.VMEM((leaf, 5 * leaf), bf16),
            pltpu.VMEM((ITERS, n * rank, outs), bf16),
            pltpu.VMEM((n * (rank + 16), rank), bf16),
            pltpu.VMEM((clusters * rank, n * rank), bf16),
            pltpu.VMEM((rank, n * rank), bf16),
            pltpu.VMEM((rank, clusters * rank), bf16),
            pltpu.VMEM((rank, clusters * rank), bf16),
            pltpu.VMEM((ITERS, rank, outs), bf16),
            pltpu.VMEM((ITERS, rank, outs), bf16),
            pltpu.VMEM((leaf, rank), bf16),
            pltpu.VMEM((rank, leaf), bf16),
            pltpu.VMEM((leaf, outs), f32),
            pltpu.VMEM((leaf, outs), f32),
            sem((stages, 5, PARTS)),
            sem((stages, 5, PARTS)),
            sem((stages, n // 2)),
            sem((stages, n // 2)),
            sem((stages, n // 2)),
            sem((stages, n // 2)),
            sem((stages,)),
            sem((stages,)),
        ],
        compiler_params=pltpu.CompilerParams(
            collective_id=0, has_side_effects=True, vmem_limit_bytes=48 << 20
        ),
        name="fused_solve",
    )(
        coords.T,
        right_side,
        leaf_perm,
        near_list,
        far_leaves,
        couplings,
        transfer,
        leaf_basis,
        cluster_of,
        far_clusters,
        cluster_couplings,
        ridge_weight.reshape(1, 1),
    )


def solution(mesh):
    fits = mesh.shape["grp"] == 2 and mesh.shape["dev"] % 4 == 0
    placed = (
        P(("grp", "dev"), None),
        P(("grp", "dev"), None),
        P(("grp", "dev"), None),
        P(("grp", "dev"), None),
        P(("grp", "dev"), None),
        P(("grp", "dev"), None, None, None),
        P(("grp", "dev"), None, None),
        P(("grp", "dev"), None),
        P(("grp", "dev")),
        P("grp", None),
        P("grp", None, None, None),
        P(),
    )
    return jax.shard_map(
        fused_body if fits else body,
        mesh=mesh,
        in_specs=placed,
        out_specs=(P(("grp", "dev"), None), P(("grp", "dev"), None)),
        check_vma=False,
    )
```
